32 devices in a mesh: shard: 8 (over y, x, core), rep: 4 (over z).
Axes of the slice: x: 2, y: 2, z: 4, core: 2. Of those that a mesh axis runs over, the one named last changes fastest.
Arguments:
- inputs: bfloat16 [64, 256, 1024], P(('shard', 'rep')), may hold values from -6 to 6
- lengths: int32 [64], replicated, may hold values from 64 to 256, as said below
- dealing: int32 [64], replicated, may hold values from 0 to 63, as said below
- w_query: bfloat16 [1024, 1024], P('shard'), may hold values from -0.25 to 0.25
- w_key: bfloat16 [1024, 1024], P('shard'), may hold values from -0.25 to 0.25
- w_value: bfloat16 [1024, 1024], P('shard'), may hold values from -0.1875 to 0.1875
- w_out: bfloat16 [1024, 1024], P('shard'), may hold values from -0.5 to 0.5
- b_query: bfloat16 [1024], P('shard'), may hold values from -1.5 to 1.5
- b_value: bfloat16 [1024], P('shard'), may hold values from -1.5 to 1.5
- b_out: bfloat16 [1024], P('shard'), may hold values from -1.5 to 1.5
- ln1_gain: bfloat16 [1024], P('shard'), may hold values from 0.099609375 to 1.8984375
- ln1_bias: bfloat16 [1024], P('shard'), may hold values from -1.5 to 1.5
- w_up: bfloat16 [1024, 4096], P('shard'), may hold values from -0.1875 to 0.1875
- b_up: bfloat16 [4096], P('shard'), may hold values from -1.5 to 1.5
- w_down: bfloat16 [4096, 1024], P('shard'), may hold values from -0.09375 to 0.09375
- b_down: bfloat16 [1024], P('shard'), may hold values from -1.5 to 1.5
- ln2_gain: bfloat16 [1024], P('shard'), may hold values from 0.099609375 to 1.8984375
- ln2_bias: bfloat16 [1024], P('shard'), may hold values from -1.5 to 1.5
- cotangent: bfloat16 [64, 256, 1024], P(('shard', 'rep')), may hold values from -6 to 6
Outputs:
- layer_out: bfloat16 [64, 256, 1024], P(('shard', 'rep'))
- grad_input: bfloat16 [64, 256, 1024], P(('shard', 'rep'))
- grad_w_query: float32 [1024, 1024], P('shard')
- grad_w_key: float32 [1024, 1024], P('shard')
- grad_w_value: float32 [1024, 1024], P('shard')
- grad_w_out: float32 [1024, 1024], P('shard')
- grad_b_query: float32 [1024], P('shard')
- grad_b_value: float32 [1024], P('shard')
- grad_b_out: float32 [1024], P('shard')
- grad_ln1_gain: float32 [1024], P('shard')
- grad_ln1_bias: float32 [1024], P('shard')
- grad_w_up: float32 [1024, 4096], P('shard')
- grad_b_up: float32 [4096], P('shard')
- grad_w_down: float32 [4096, 1024], P('shard')
- grad_b_down: float32 [1024], P('shard')
- grad_ln2_gain: float32 [1024], P('shard')
- grad_ln2_bias: float32 [1024], P('shard')
The draws below stay inside these ranges and needn't reach their ends.
Inputs may be any that keep to these rules, and one draw needn't show every extreme that they name: `lengths`: length of initial sequence; positions at or past it are padding. `dealing`: a permutation of the 64 sequences that maps each aligned block of 8 positions onto itself.
All inputs are finite; a program needn't handle non-finite values.
Results may differ from the reference program's by a relative error of at most 0.02.
Values may be sent and summed in bfloat16 or wider, within the bound.
No kernel may reach another device: no remote copies, remote signals or barrier semaphores. Data moves between devices by JAX's collectives and lax.ppermute only.
A program may use at most 192 MiB of HBM per device.

```python
import jax
import jax.numpy as jnp
from jax import lax

D = 1024
H = 16
HD = 64
FF = 4096
SLOT = 256
MB = 2
GROUP = 8
SEQS = 64


def common_lengths(key):
    inner = jax.random.fold_in(key, 11)
    first, second, third = jax.random.split(inner, 3)
    drawn = jax.random.randint(first, (SEQS,), SLOT // 4, SLOT + 1, dtype=jnp.int32)
    high_at = jax.random.randint(second, (), 0, SEQS, dtype=jnp.int32)
    short_at = (high_at + 1 + jax.random.randint(third, (), 0, SEQS - 1, dtype=jnp.int32)) % SEQS
    spots = jnp.arange(SEQS, dtype=jnp.int32)
    drawn = jnp.where(spots == high_at, SLOT, drawn)
    drawn = jnp.where(spots == short_at, SLOT // 4, drawn)
    return drawn


def draw_lengths(key, part):
    return common_lengths(key)


def draw_dealing(key, part):
    lengths = common_lengths(key)
    blocks = SEQS // GROUP
    replicas = GROUP // MB
    grouped = lengths.reshape(blocks, GROUP)
    places = jnp.arange(GROUP, dtype=jnp.int32)
    score = grouped * GROUP + (GROUP - 1 - places)[None, :]
    order = jnp.argsort(-score, axis=1, stable=True).astype(jnp.int32)
    rounds = places // replicas
    within = places % replicas
    device = jnp.where(rounds % 2 == 0, within, replicas - 1 - within)
    target = device * MB + rounds
    starts = (jnp.arange(blocks, dtype=jnp.int32) * GROUP)[:, None]
    placed = jnp.zeros((blocks, GROUP), jnp.int32).at[:, target].set(order + starts)
    return placed.reshape(SEQS)


def level_of(key, shape, cuts, smallest, high):
    level = 1.0
    for dim, shards_of in cuts:
        steps = jax.random.uniform(jax.random.fold_in(jax.random.fold_in(key, 6), dim), (shards_of,), jnp.float32, smallest / len(cuts), high / len(cuts))
        level = level * jnp.repeat(jnp.exp(steps), shape[dim] // shards_of).reshape((-1,) + (1,) * (len(shape) - 1 - dim))
    return level


def noise(stream_key, dims, deviation, bound, cuts=(), kind=jnp.bfloat16):
    values = deviation * jax.random.normal(stream_key, dims, jnp.float32)
    if cuts:
        values = values * level_of(stream_key, dims, cuts, -0.22, 0.18)
    return jnp.clip(values, -bound, bound).astype(kind)


def setup_inputs(seed: int = 0) -> dict:
    keys = jax.random.split(jax.random.key(seed), 20)
    return {
        "inputs": noise(keys[0], (SEQS, SLOT, D), 1.0, 6.0, ((0, 32),)),
        "lengths": draw_lengths(jax.random.fold_in(keys[19], 71), 0),
        "dealing": draw_dealing(jax.random.fold_in(keys[19], 71), 0),
        "w_query": noise(keys[3], (D, D), (D // 2) ** -0.5, 0.25, ((0, 8),)),
        "w_key": noise(keys[4], (D, D), (D // 2) ** -0.5, 0.25, ((0, 8),)),
        "w_value": noise(keys[5], (D, D), D ** -0.5, 0.1875, ((0, 8),)),
        "w_out": noise(keys[6], (D, D), (D // 8) ** -0.5, 0.5, ((0, 8),)),
        "b_query": noise(keys[7], (D,), 0.3, 1.5, ((0, 8),)),
        "b_value": noise(keys[8], (D,), 0.3, 1.5, ((0, 8),)),
        "b_out": noise(keys[9], (D,), 0.3, 1.5, ((0, 8),)),
        "ln1_gain": jnp.clip(1.0 + 0.18 * jax.random.normal(keys[10], (D,), jnp.float32), 0.099609375, 1.8984375).astype(jnp.bfloat16),
        "ln1_bias": noise(keys[11], (D,), 0.3, 1.5, ((0, 8),)),
        "w_up": noise(keys[12], (D, FF), D ** -0.5, 0.1875, ((0, 8),)),
        "b_up": noise(keys[13], (FF,), 0.3, 1.5, ((0, 8),)),
        "w_down": noise(keys[14], (FF, D), FF ** -0.5, 0.09375, ((0, 8),)),
        "b_down": noise(keys[15], (D,), 0.3, 1.5, ((0, 8),)),
        "ln2_gain": jnp.clip(1.0 + 0.18 * jax.random.normal(keys[16], (D,), jnp.float32), 0.099609375, 1.8984375).astype(jnp.bfloat16),
        "ln2_bias": noise(keys[17], (D,), 0.3, 1.5, ((0, 8),)),
        "cotangent": noise(keys[18], (SEQS, SLOT, D), 1.0, 6.0, ((0, 32),)),
    }


EPS = 1e-05
NEG = -1e+30
HIGHEST = lax.Precision.HIGHEST

@jax.custom_vjp
def low(v):
    return lax.optimization_barrier(v.astype(jnp.bfloat16)).astype(jnp.float32)

@jax.custom_vjp
def low_back(v):
    return v

def low_keep(v):
    return (low(v), None)

def low_pass(kept, grad):
    return (grad,)

def back_keep(v):
    return (v, None)

def back_low(kept, grad):
    return (low(grad),)
low.defvjp(low_keep, low_pass)
low_back.defvjp(back_keep, back_low)

def product(left, right):
    return jnp.dot(left, right, precision=HIGHEST, preferred_element_type=jnp.float32)

def norm_rows(values, gain, shift):
    center = values - lax.optimization_barrier(jnp.mean(values, -1, keepdims=True))
    spread = lax.optimization_barrier(jnp.mean(center * center, -1, keepdims=True))
    return center * lax.rsqrt(spread + EPS) * gain + shift

def layer_block(tokens, seq_lens, params):
    w_query, w_key, w_value, w_out, b_query, b_value, b_out, ln1_gain, ln1_bias, w_up, b_up, w_down, b_down, ln2_gain, ln2_bias = params
    count, rows, width = tokens.shape
    query = low(low_back(product(tokens, w_query) + b_query)).reshape(count, rows, H, HD)
    keyed = low(low_back(product(tokens, w_key))).reshape(count, rows, H, HD)
    value = low(low_back(product(tokens, w_value) + b_value)).reshape(count, rows, H, HD)
    raw = jnp.einsum('bqhd,bkhd->bhqk', query, keyed, precision=HIGHEST)
    scores = low_back(raw) * HD ** (-0.5)
    places = jnp.arange(rows)
    allowed = places[None, None, None, :] < seq_lens[:, None, None, None]
    scores = jnp.where(allowed, scores, NEG)
    probs = jax.nn.softmax(scores, axis=-1)
    mixed = jnp.einsum('bhqk,bkhd->bqhd', low(probs), value, precision=HIGHEST).reshape(count, rows, width)
    branch = low_back(product(low(low_back(mixed)), w_out)) + b_out
    hidden = norm_rows(tokens + branch, ln1_gain, ln1_bias)
    pre = low_back(product(low(hidden), w_up) + b_up)
    act = low(jax.nn.gelu(pre, approximate=False))
    summed = hidden + low_back(product(act, w_down)) + b_down
    normed = norm_rows(summed, ln2_gain, ln2_bias)
    rows_ok = places[None, :] < seq_lens[:, None]
    return jnp.where(rows_ok[..., None], normed, 0.0)

def reference(inputs, lengths, dealing, w_query, w_key, w_value, w_out, b_query, b_value, b_out, ln1_gain, ln1_bias, w_up, b_up, w_down, b_down, ln2_gain, ln2_bias, cotangent):
    params = tuple((item.astype(jnp.float32) for item in (w_query, w_key, w_value, w_out, b_query, b_value, b_out, ln1_gain, ln1_bias, w_up, b_up, w_down, b_down, ln2_gain, ln2_bias)))
    dealt = jnp.take(inputs, dealing, axis=0).astype(jnp.float32)
    seq_lens = jnp.take(lengths, dealing, axis=0)
    per_block = max(1, min(SEQS, 4096 // SLOT))
    blocks = SEQS // per_block

    def whole(tokens, weights):

        def one_block(pair):
            return layer_block(pair[0], pair[1], weights)
        outs = lax.map(jax.checkpoint(one_block), (tokens.reshape(blocks, per_block, SLOT, D), seq_lens.reshape(blocks, per_block)))
        return outs.reshape(SEQS, SLOT, D)
    layer_out, pull = jax.vjp(whole, dealt, params)
    grad_dealt, grads = pull(cotangent.astype(jnp.float32))
    grad_input = jnp.zeros_like(grad_dealt).at[dealing].set(grad_dealt)
    g_wq, g_wk, g_wv, g_wo, g_bq, g_bv, g_bo, g_l1g, g_l1b, g_wu, g_bu, g_wd, g_bd, g_l2g, g_l2b = grads
    return (layer_out.astype(jnp.bfloat16), grad_input.astype(jnp.bfloat16), g_wq, g_wk, g_wv, g_wo, g_bq, g_bv, g_bo, g_l1g, g_l1b, g_wu, g_bu, g_wd, g_bd, g_l2g, g_l2b)
```

```python
import functools

import jax
import jax.numpy as jnp
from jax import lax
from jax.experimental import pallas as pl
from jax.experimental.pallas import tpu as pltpu
from jax.sharding import PartitionSpec as P

H = 16
HD = 64
EPS = 1e-05
NEG = -1e30
F32 = jnp.float32
BF16 = jnp.bfloat16


def matmul(left, right):
    return jnp.dot(left, right, preferred_element_type=F32)


def left_trans(left, right):
    return lax.dot_general(left, right, (((0,), (0,)), ((), ())), preferred_element_type=F32)


def right_trans(left, right):
    return lax.dot_general(left, right, (((1,), (1,)), ((), ())), preferred_element_type=F32)


def cost(flops, nbytes):
    return pl.CostEstimate(flops=int(flops), bytes_accessed=int(nbytes), transcendentals=0)


ANY = pl.BlockSpec(memory_space=pl.ANY)
WHOLE = pl.BlockSpec(memory_space=pltpu.VMEM)
SCALAR = pl.BlockSpec(memory_space=pltpu.SMEM)


def swap(array, mask, axis="shard"):
    count = lax.axis_size(axis)
    return lax.ppermute(array, axis, [(i, i ^ mask) for i in range(count)])


def spread(own, first):
    second = 6 ^ first
    pieces = [None] * 8
    pieces[0] = own
    pieces[first] = swap(own, first)
    pieces[second] = swap(own, second)
    pieces[6] = swap(pieces[first], second)
    for mask in (0, first, second, 6):
        pieces[mask ^ 1] = swap(pieces[mask], 1)
    return pieces


def assemble_kernel(places, count, mine_ref, *refs):
    pieces, out, sem = refs[:count], refs[count], refs[count + 1]
    copies = []
    for number, (mask, source, start, rows, size, base) in enumerate(places):
        index = mine_ref[0] ^ mask
        offset = pl.multiple_of(index * size + base, rows)
        copies.append(
            pltpu.make_async_copy(
                pieces[source].at[pl.ds(start, rows)], out.at[pl.ds(offset, rows)], sem.at[number]
            )
        )
    for copy in copies:
        copy.start()
    for copy in copies:
        copy.wait()


def assemble(mine, pieces, places, shape):
    return pl.pallas_call(
        functools.partial(assemble_kernel, tuple(places), len(pieces)),
        out_shape=jax.ShapeDtypeStruct(shape, BF16),
        in_specs=[SCALAR] + [ANY] * len(pieces),
        out_specs=WHOLE,
        scratch_shapes=[pltpu.SemaphoreType.DMA((len(places),))],
        cost_estimate=cost(0, 4 * shape[0] * shape[1]),
        name="assemble",
    )(mine, *pieces)


def grad_send_kernel(count, block, extra, parts, mine_ref, left_ref, *refs):
    rights, refs = refs[:parts], refs[parts:]
    if extra:
        vec_ref, refs = refs[0], refs[1:]
    out_ref = refs[0]
    for place in range(count // 2):
        index = mine_ref[0] ^ (2 * place + 1)
        left = left_ref[:, pl.ds(pl.multiple_of(index * block, block), block)]
        start = 0
        for right in rights:
            width = right.shape[1]
            out_ref[place, :block, start : start + width] = left_trans(left, right[...]).astype(
                BF16
            )
            start += width
        if extra:
            out_ref[place, block:, :] = vec_ref[index].astype(BF16)


def grad_own_kernel(count, block, extra, parts, mine_ref, left_ref, *refs):
    rights, refs = refs[:parts], refs[parts:]
    if extra:
        vec_ref, refs = refs[0], refs[1:]
    recv_ref, outs = refs[0], refs[1:]
    half = block // 2
    for place in (3, 1, 2, 0):
        index = mine_ref[0] ^ (2 * place)
        left = left_ref[:, pl.ds(pl.multiple_of(index * block, block), block)]
        start = 0
        for right in rights:
            width = right.shape[1]
            cols = slice(start, start + width)
            value = left_trans(left, right[...]) + recv_ref[place, :block, cols].astype(F32)
            if place == 0:
                outs[0][:block, cols] = value
            else:
                outs[2 * place - 1][:, cols] = value[:half].astype(BF16)
                outs[2 * place][:half, cols] = value[half:].astype(BF16)
            start += width
        if extra:
            value = vec_ref[index] + recv_ref[place, block:, :].astype(F32)
            if place == 0:
                outs[0][block:, :] = value
            else:
                outs[2 * place][half:, :] = value.astype(BF16)


def grad_blocks(mine, left, rights, vec=None):
    count = lax.axis_size("shard")
    tokens, width = left.shape
    block = width // count
    extra = 0 if vec is None else vec.shape[1]
    columns = sum(r.shape[1] for r in rights)
    flops = tokens * width * columns
    send = pl.pallas_call(
        functools.partial(grad_send_kernel, count, block, extra, len(rights)),
        out_shape=jax.ShapeDtypeStruct((count // 2, block + extra, columns), BF16),
        in_specs=[SCALAR] + [WHOLE] * (1 + len(rights) + (vec is not None)),
        out_specs=WHOLE,
        cost_estimate=cost(flops, 2 * (tokens * (width + columns) + width * columns // 2)),
        name="grad_send",
    )(mine, left, *rights, *([] if vec is None else [vec]))
    recv = swap(send, 1)
    half = block // 2
    shapes = [jax.ShapeDtypeStruct((block + extra, columns), F32)]
    for _ in range(3):
        shapes.append(jax.ShapeDtypeStruct((half, columns), BF16))
        shapes.append(jax.ShapeDtypeStruct((half + extra, columns), BF16))
    return pl.pallas_call(
        functools.partial(grad_own_kernel, count, block, extra, len(rights)),
        out_shape=shapes,
        in_specs=[SCALAR] + [WHOLE] * (2 + len(rights) + (vec is not None)),
        out_specs=[WHOLE] * 7,
        cost_estimate=cost(flops, 2 * (tokens * (width + columns) + width * columns)),
        name="grad_own",
    )(mine, left, *rights, *([] if vec is None else [vec]), recv)


def add_low(left, right):
    return (left.astype(F32) + right.astype(F32)).astype(BF16)


def reduce_blocks(blocks):
    own, x_top, x_low, y_top, y_low, d_top, d_low = blocks
    half = x_top.shape[0]
    from_x = swap(x_top, 2)
    from_y = swap(y_low, 4)
    y_top = add_low(y_top, swap(d_top, 2))
    x_low = add_low(x_low, swap(d_low, 4))
    top = own[:half] + from_x.astype(F32) + swap(y_top, 4).astype(F32)
    low = own[half:] + from_y.astype(F32) + swap(x_low, 2).astype(F32)
    return jnp.concatenate([top, low]).astype(BF16)


def over_rep(own):
    rep = lax.axis_index("rep")
    middle = add_low(own, lax.ppermute(own, "rep", [(0, 1), (3, 2)]))
    both = add_low(middle, lax.ppermute(middle, "rep", [(1, 2), (2, 1)]))
    back = lax.ppermute(both, "rep", [(1, 0), (2, 3)])
    return jnp.where((rep == 1) | (rep == 2), both, back)


def choose_kernel(count, which_ref, slot_ref, *refs):
    arrays, out, sem = refs[:count], refs[count], refs[count + 1]
    for place in range(out.shape[0]):
        for number in range(count):

            @pl.when(which_ref[place] == number)
            def _(place=place, number=number):
                pltpu.make_async_copy(
                    arrays[number].at[slot_ref[place]], out.at[place], sem.at[place]
                ).start()

    for place in range(out.shape[0]):
        pltpu.make_async_copy(arrays[0].at[0], out.at[place], sem.at[place]).wait()


def choose(arrays, which, slot):
    shape = arrays[0].shape
    return pl.pallas_call(
        functools.partial(choose_kernel, len(arrays)),
        out_shape=jax.ShapeDtypeStruct(shape, arrays[0].dtype),
        in_specs=[SCALAR, SCALAR] + [ANY] * len(arrays),
        out_specs=WHOLE,
        scratch_shapes=[pltpu.SemaphoreType.DMA((shape[0],))],
        cost_estimate=cost(0, 4 * shape[0] * shape[1] * shape[2]),
        name="choose",
    )(which, slot, *arrays)


def route(values, source):
    batches = values.shape[0]
    rep = lax.axis_index("rep")
    left1 = lax.ppermute(values, "rep", [(2, 1), (3, 2)])
    right1 = lax.ppermute(values, "rep", [(1, 2), (0, 1)])
    left2 = lax.ppermute(left1, "rep", [(2, 1)])
    right2 = lax.ppermute(right1, "rep", [(1, 2)])
    arrays = [values, left1, left2, right1, right2]
    slots = jnp.arange(batches, dtype=jnp.int32)

    def place_of(wanted, at):
        apart = wanted // batches - at
        which = jnp.where(
            apart == 0,
            0,
            jnp.where(apart == 1, 1, jnp.where(apart >= 2, 2, jnp.where(apart == -1, 3, 4))),
        )
        return which.astype(jnp.int32), (wanted % batches).astype(jnp.int32)

    outer = jnp.where(rep <= 1, 0, 3)
    which, slot = place_of(jnp.take(source, outer * batches + slots), rep)
    passed = choose(arrays, which, slot)
    last = lax.ppermute(passed, "rep", [(1, 0), (2, 3)])
    wanted = jnp.take(source, rep * batches + slots)
    which, slot = place_of(wanted, rep)
    edge = (rep == 0) | (rep == 3)
    relayed = edge & (which != 0)
    return choose(
        arrays + [last], jnp.where(relayed, 5, which), jnp.where(relayed, slots, slot)
    )


def gathered(values, source):
    batches = values.shape[0]
    rep = lax.axis_index("rep")
    whole = lax.all_gather(values, "rep", axis=0, tiled=True)
    return jnp.take(whole, jnp.take(source, rep * batches + jnp.arange(batches)), axis=0)


def head_mask(dtype):
    lane = lax.broadcasted_iota(jnp.int32, (1, 2 * HD), 1)
    return [(lane < HD).astype(F32).astype(dtype), (lane >= HD).astype(F32).astype(dtype)]


def attend_kernel(len_ref, q_ref, k_ref, v_ref, mixed_ref, probs_ref):
    length = len_ref[pl.program_id(0)]
    rows = q_ref.shape[0]
    allowed = lax.broadcasted_iota(jnp.int32, (rows, rows), 1) < length
    masks = head_mask(BF16)
    query, keyed, value = q_ref[...], k_ref[...], v_ref[...]
    mixed = []
    for head in range(2):
        scores = right_trans(query * masks[head], keyed) * (HD**-0.5)
        scores = jnp.where(allowed, scores, NEG)
        peak = jnp.max(scores, -1, keepdims=True)
        raised = jnp.exp(scores - peak)
        probs = (raised / jnp.sum(raised, -1, keepdims=True)).astype(BF16)
        probs_ref[0, head] = probs
        mixed.append(matmul(probs, value))
    lane = lax.broadcasted_iota(jnp.int32, mixed[0].shape, 1)
    mixed_ref[...] = jnp.where(lane < HD, mixed[0], mixed[1]).astype(BF16)


def attend(query, keyed, value, lengths, rows):
    count = lengths.shape[0]
    block = pl.BlockSpec((rows, 2 * HD), lambda b, h, *_: (b, h))
    return pl.pallas_call(
        attend_kernel,
        out_shape=[
            jax.ShapeDtypeStruct(query.shape, BF16),
            jax.ShapeDtypeStruct((count, H, rows, rows), BF16),
        ],
        grid_spec=pltpu.PrefetchScalarGridSpec(
            num_scalar_prefetch=1,
            grid=(count, H // 2),
            in_specs=[block] * 3,
            out_specs=[block, pl.BlockSpec((1, 2, rows, rows), lambda b, h, *_: (b, h, 0, 0))],
        ),
        cost_estimate=cost(
            count * H * rows * rows * 4 * 128, 8 * query.size + 2 * count * H * rows * rows
        ),
        name="attend",
    )(lengths, query, keyed, value)


def attend_back_kernel(q_ref, k_ref, v_ref, g_ref, probs_ref, gq_ref, gk_ref, gv_ref):
    masks = head_mask(BF16)
    query, keyed, value, grad = q_ref[...], k_ref[...], v_ref[...], g_ref[...]
    outs = [[], [], []]
    for head in range(2):
        low = probs_ref[0, head]
        probs = low.astype(F32)
        grad_probs = right_trans(grad * masks[head], value)
        inner = jnp.sum(probs * grad_probs, -1, keepdims=True)
        scores = (probs * (grad_probs - inner) * (HD**-0.5)).astype(BF16)
        outs[0].append(matmul(scores, keyed))
        outs[1].append(left_trans(scores, query))
        outs[2].append(left_trans(low, grad))
    lane = lax.broadcasted_iota(jnp.int32, outs[0][0].shape, 1)
    for ref, (first, second) in zip((gq_ref, gk_ref, gv_ref), outs):
        ref[...] = jnp.where(lane < HD, first, second).astype(BF16)


def attend_back(query, keyed, value, grad_mixed, probs):
    count, _, rows, _ = probs.shape
    block = pl.BlockSpec((rows, 2 * HD), lambda b, h: (b, h))
    return pl.pallas_call(
        attend_back_kernel,
        out_shape=[jax.ShapeDtypeStruct(query.shape, BF16)] * 3,
        grid=(count, H // 2),
        in_specs=[block] * 4 + [pl.BlockSpec((1, 2, rows, rows), lambda b, h: (b, h, 0, 0))],
        out_specs=[block] * 3,
        cost_estimate=cost(
            count * H * rows * rows * 8 * 128, 14 * query.size + 2 * count * H * rows * rows
        ),
        name="attend_back",
    )(query, keyed, value, grad_mixed, probs)


def normalize(values):
    center = values - jnp.mean(values, -1, keepdims=True)
    inverse = lax.rsqrt(jnp.mean(center * center, -1, keepdims=True) + EPS)
    return center * inverse, inverse


def norm_back(grad, unit, inverse, gain):
    scaled = grad * gain
    return inverse * (
        scaled
        - jnp.mean(scaled, -1, keepdims=True)
        - unit * jnp.mean(scaled * unit, -1, keepdims=True)
    )


def gelu_both(pre):
    cumul = 0.5 * (1.0 + lax.erf(pre * 0.7071067811865476))
    density = jnp.exp(-0.5 * pre * pre) * 0.3989422804014327
    return (pre * cumul, cumul + pre * density)


def local(
    inputs,
    lengths,
    dealing,
    w_query,
    w_key,
    w_value,
    w_out,
    b_query,
    b_value,
    b_out,
    ln1_gain,
    ln1_bias,
    w_up,
    b_up,
    w_down,
    b_down,
    ln2_gain,
    ln2_bias,
    cotangent,
):
    batches, rows, width = inputs.shape
    shards = lax.axis_size("shard")
    replicas = lax.axis_size("rep")
    group = batches * replicas
    shard_index = lax.axis_index("shard")
    rep_index = lax.axis_index("rep")
    anchor = shard_index * group
    mine = shard_index.astype(jnp.int32).reshape(1)
    places = jnp.arange(group, dtype=jnp.int32)
    slots = (shard_index * replicas + rep_index) * batches + jnp.arange(batches, dtype=jnp.int32)
    seq_lengths = jnp.take(lengths, slots)
    dealt_from = lax.dynamic_slice_in_dim(dealing, anchor, group) - anchor
    dealt_to = jnp.sum(
        jnp.where(dealt_from[None, :] == places[:, None], places[None, :], 0), 1, dtype=jnp.int32
    )
    tokens = inputs.reshape(batches * rows, width)
    fast = shards == 8
    mover = route if replicas == 4 else gathered

    vec = jnp.concatenate(
        [b_query, b_value, b_out, ln1_gain, ln1_bias, b_down, ln2_gain, ln2_bias, b_up]
    )
    small = width // shards
    hidden_small = b_up.shape[0]
    if fast:
        vec_rows = jnp.zeros((16 * width,), BF16).at[: vec.shape[0]].set(vec).reshape(16, width)
        split = small // 2
        first = spread(jnp.concatenate([w_query, w_key[:split], vec_rows]), 2)
        second = spread(jnp.concatenate([w_key[split:], w_value]), 4)
        out_pieces = spread(w_out, 2)
        up_half, down_half = w_up.shape[0] // 2, w_down.shape[0] // 2
        ups = spread(w_up[:up_half], 4) + spread(w_up[up_half:], 2)
        downs = spread(w_down[:down_half], 4) + spread(w_down[down_half:], 2)
        square = (width, width)
        full_query = assemble(mine, first, [(m, m, 0, small, small, 0) for m in range(8)], square)
        full_key = assemble(
            mine,
            first + second,
            [(m, m, small, split, small, 0) for m in range(8)]
            + [(m, m + 8, 0, split, small, split) for m in range(8)],
            square,
        )
        full_value = assemble(
            mine, second, [(m, m, split, small, small, 0) for m in range(8)], square
        )
        full_out = assemble(
            mine, out_pieces, [(m, m, 0, small, small, 0) for m in range(8)], square
        )

        def two_halves(pieces, half):
            return assemble(
                mine,
                pieces,
                [(m, m, 0, half, 2 * half, 0) for m in range(8)]
                + [(m, m + 8, 0, half, 2 * half, half) for m in range(8)],
                (16 * half, pieces[0].shape[1]),
            )

        full_up = two_halves(ups, up_half)
        full_down = two_halves(downs, down_half)
        vecs = jnp.stack([p[small + split :].reshape(-1)[: vec.shape[0]] for p in first])
        vecs = jnp.take(vecs, mine ^ jnp.arange(8, dtype=jnp.int32), axis=0)
    else:
        full_query, full_key, full_value, full_out, full_up, full_down = (
            lax.all_gather(w, "shard", axis=0, tiled=True)
            for w in (w_query, w_key, w_value, w_out, w_up, w_down)
        )
        vecs = lax.all_gather(vec, "shard", axis=0)
    vecs = vecs.astype(F32)
    bias_query, bias_value, bias_out, gain_one, shift_one, bias_down, gain_two, shift_two = (
        vecs[:, n * small : (n + 1) * small].reshape(1, width) for n in range(8)
    )
    bias_up = vecs[:, 8 * small :].reshape(1, -1)

    cot = mover(cotangent, dealt_to).reshape(batches * rows, width)
    query = (matmul(tokens, full_query) + bias_query).astype(BF16)
    keyed = matmul(tokens, full_key).astype(BF16)
    value = (matmul(tokens, full_value) + bias_value).astype(BF16)
    mixed, probs = attend(query, keyed, value, seq_lengths, rows)
    unit_one, inverse_one = normalize(tokens.astype(F32) + matmul(mixed, full_out) + bias_out)
    hidden = unit_one * gain_one + shift_one
    hidden_low = hidden.astype(BF16)
    act, slope = gelu_both(matmul(hidden_low, full_up) + bias_up)
    act = act.astype(BF16)
    slope = slope.astype(BF16)
    unit_two, inverse_two = normalize(hidden + matmul(act, full_down) + bias_down)
    valid = (
        lax.broadcasted_iota(jnp.int32, (batches, rows, 1), 1) < seq_lengths[:, None, None]
    ).reshape(batches * rows, 1)
    out = jnp.where(valid, unit_two * gain_two + shift_two, 0.0).astype(BF16)
    layer_out = mover(out.reshape(inputs.shape), dealt_from)

    grad_out = jnp.where(valid, cot.astype(F32), 0.0)
    g_gain_two = jnp.sum(grad_out * unit_two, 0)
    g_shift_two = jnp.sum(grad_out, 0)
    grad_sum = norm_back(grad_out, unit_two, inverse_two, gain_two)
    g_bdown = jnp.sum(grad_sum, 0)
    grad_sum_low = grad_sum.astype(BF16)
    grad_pre = (right_trans(grad_sum_low, full_down) * slope.astype(F32)).astype(BF16)
    g_bup = jnp.sum(grad_pre.astype(F32), 0)
    grad_hidden = grad_sum + right_trans(grad_pre, full_up)
    g_gain_one = jnp.sum(grad_hidden * unit_one, 0)
    g_shift_one = jnp.sum(grad_hidden, 0)
    grad_resid = norm_back(grad_hidden, unit_one, inverse_one, gain_one)
    g_bout = jnp.sum(grad_resid, 0)
    grad_resid_low = grad_resid.astype(BF16)
    grad_mixed = right_trans(grad_resid_low, full_out).astype(BF16)
    g_query, g_key, g_value = attend_back(query, keyed, value, grad_mixed, probs)
    g_bquery = jnp.sum(g_query.astype(F32), 0)
    g_bvalue = jnp.sum(g_value.astype(F32), 0)
    grad_input = (
        grad_resid
        + right_trans(g_query, full_query)
        + right_trans(g_key, full_key)
        + right_trans(g_value, full_value)
    ).astype(BF16)

    g_vec = jnp.concatenate(
        [
            part.reshape(shards, -1)
            for part in (
                g_bquery,
                g_bvalue,
                g_bout,
                g_gain_one,
                g_shift_one,
                g_bdown,
                g_gain_two,
                g_shift_two,
                g_bup,
            )
        ],
        1,
    )
    if fast:
        spare = jnp.zeros((shards, 16, 3 * width), F32)
        spare = spare.at[:, 0, : g_vec.shape[1]].set(g_vec)
        g_wdown = reduce_blocks(grad_blocks(mine, act, [grad_sum_low]))
        g_wup = reduce_blocks(grad_blocks(mine, hidden_low, [grad_pre]))
        g_wout = reduce_blocks(grad_blocks(mine, mixed, [grad_resid_low]))
        g_rest = reduce_blocks(grad_blocks(mine, tokens, [g_query, g_key, g_value], spare))
        g_wdown, g_wup, g_wout, g_rest = (over_rep(g) for g in (g_wdown, g_wup, g_wout, g_rest))
        g_wdown, g_wup, g_wout, g_rest = (g.astype(F32) for g in (g_wdown, g_wup, g_wout, g_rest))
        g_wquery, g_wkey, g_wvalue = (g_rest[:small, n * width : (n + 1) * width] for n in range(3))
        g_own = g_rest[small, : g_vec.shape[1]]
    else:

        def scattered(left, right):
            share = lax.psum_scatter(
                left_trans(left, right).astype(BF16), "shard", scatter_dimension=0, tiled=True
            )
            return lax.psum(share, "rep").astype(F32)

        g_wdown = scattered(act, grad_sum_low)
        g_wup = scattered(hidden_low, grad_pre)
        g_wout = scattered(mixed, grad_resid_low)
        g_wquery = scattered(tokens, g_query)
        g_wkey = scattered(tokens, g_key)
        g_wvalue = scattered(tokens, g_value)
        g_own = lax.psum(lax.psum_scatter(g_vec, "shard", scatter_dimension=0, tiled=False), "rep")
    parts = [g_own[n * small : (n + 1) * small] for n in range(8)]
    o_bquery, o_bvalue, o_bout, o_gain_one, o_shift_one, o_bdown, o_gain_two, o_shift_two = parts
    o_bup = g_own[8 * small : 8 * small + hidden_small]
    return (
        layer_out,
        grad_input.reshape(inputs.shape),
        g_wquery,
        g_wkey,
        g_wvalue,
        g_wout,
        o_bquery,
        o_bvalue,
        o_bout,
        o_gain_one,
        o_shift_one,
        g_wup,
        o_bup,
        g_wdown,
        o_bdown,
        o_gain_two,
        o_shift_two,
    )


def solution(mesh):
    sequences = P(("shard", "rep"), None, None)
    matrix, vector = P("shard", None), P("shard")
    in_specs = (
        (sequences, P(), P())
        + (matrix,) * 4
        + (vector,) * 5
        + (matrix, vector, matrix, vector, vector, vector, sequences)
    )
    out_specs = (
        (sequences, sequences)
        + (matrix,) * 4
        + (vector,) * 5
        + (matrix, vector, matrix, vector, vector, vector)
    )
    return jax.shard_map(local, mesh=mesh, in_specs=in_specs, out_specs=out_specs, check_vma=False)
```
